32 devices in a mesh: rep: 2 (over x), ep: 4 (over y, core), grp: 4 (over z).
Axes of the slice: x: 2, y: 2, z: 4, core: 2. Of those that a mesh axis runs over, the one named last changes fastest.
Arguments:
- tokens: bfloat16 [4096, 4096], P(('rep', 'ep'), 'grp'), parts along dimension 0, may hold values from -6 to 6
- proj_in: bfloat16 [1024, 4096], P('ep', 'grp'), may hold values from -0.09375 to 0.09375
- proj_out: bfloat16 [1024, 4096], P('ep', 'grp'), may hold values from -0.1875 to 0.1875
- expert_up: bfloat16 [16, 1024, 2688], P(('ep', 'grp')), may hold values from -0.1875 to 0.1875
- expert_down: bfloat16 [16, 2688, 1024], P(('ep', 'grp')), may hold values from -0.125 to 0.125
- expert_ids: int32 [4096, 6], P(('rep', 'ep')), parts along dimension 0, may hold values from 0 to 15, as said below
- weight_codes: int32 [4096, 6], P(('rep', 'ep')), parts along dimension 0, may hold values from 1 to 64
Outputs:
- mixed: bfloat16 [4096, 4096], P(('rep', 'ep'), 'grp'), parts along dimension 0
The draws below stay inside these ranges and needn't reach their ends.
There are 2 independent parts, one for each index of `rep`. The reference program is written for one: setup_inputs(seed, part) draws one part's arguments, and reference() takes and returns one part's arrays. A program takes and returns all parts, laid end to end along the dimension named above; an argument that names none is the same for every part. Nothing has to cross between parts.
Inputs may be any that keep to these rules, and one draw needn't show every extreme that they name: `expert_ids`: expert e belongs to group e % 4. Each token picks 6 distinct experts, two in each of 3 distinct groups. Within each aligned block of 128 tokens (the tokens of one device), every group is picked from by exactly 96 tokens, no expert is picked by more than 64 tokens, and in every block each group has an expert picked by exactly 64.
All inputs are finite; a program needn't handle non-finite values.
Results may differ from the reference program's by a relative error of at most 0.012.
Values may be sent and summed in bfloat16 or wider, within the bound.
A program may use at most 64 MiB of HBM per device.

```python
import jax
import jax.numpy as jnp
from jax import lax

D = 4096
L = 1024
FF = 2688
GROUP_HITS = 3
PICKS = 6
TOK_DEV = 128
EXPERTS = 16
MOST = 64
TOKENS = 2048
N_EP = 4
N_GRP = 4


def group_labels(key):
    key_order, key_slots = jax.random.split(key)
    group_rows = TOK_DEV * GROUP_HITS // N_GRP
    order = jax.random.permutation(key_order, jnp.arange(N_EP, dtype=jnp.int32))
    rest = 2 * group_rows - MOST
    base = rest // (N_EP - 1)
    extra = rest % (N_EP - 1)
    ranks = jnp.arange(N_EP, dtype=jnp.int32)
    counts = jnp.where(ranks == 0, MOST, base + (ranks - 1 < extra).astype(jnp.int32)).astype(jnp.int32)
    labels = jnp.repeat(order, counts, total_repeat_length=2 * group_rows)
    slot_perm = jax.random.permutation(key_slots, jnp.arange(group_rows, dtype=jnp.int32))
    return (labels, slot_perm)


def block_ids(key):
    key_start, key_groups = jax.random.split(key)
    group_rows = TOK_DEV * GROUP_HITS // N_GRP
    starts = jax.random.permutation(key_start, jnp.arange(TOK_DEV, dtype=jnp.int32) % N_GRP)
    groups = (starts[:, None] + jnp.arange(GROUP_HITS, dtype=jnp.int32)[None, :]) % N_GRP
    hit = jnp.any(groups[:, :, None] == jnp.arange(N_GRP, dtype=jnp.int32), axis=1).astype(jnp.int32)
    rank_all = jnp.cumsum(hit, axis=0) - hit
    rank = jnp.take_along_axis(rank_all, groups, axis=1)
    labels, slot_perm = jax.vmap(group_labels)(jax.random.split(key_groups, N_GRP))
    slot = slot_perm[groups, rank]
    first = labels[groups, slot]
    second = labels[groups, slot + group_rows]
    members = jnp.stack([first, second], axis=2)
    ids = members * N_GRP + groups[:, :, None]
    return ids.reshape(TOK_DEV, 2 * GROUP_HITS).astype(jnp.int32)


def draw_expert_ids(key, part):
    blocks = TOKENS // TOK_DEV
    keys = jax.random.split(jax.random.fold_in(key, 7), blocks)
    return jax.vmap(block_ids)(keys).reshape(TOKENS, PICKS)


def plant(values, own_key, low, largest):
    longest = values.shape.index(max(values.shape))
    spots = []
    for shift in (0, 1):
        where = [jax.random.randint(jax.random.fold_in(own_key, axis), (), 0, length) for axis, length in enumerate(values.shape)]
        where[longest] = (where[longest] + shift) % values.shape[longest]
        spots.append(tuple(where))
    return values.at[spots[0]].set(low).at[spots[1]].set(largest)


def shard_levels(stream_key, dims, cuts, smallest, largest):
    level, own = 1.0, jax.random.fold_in(stream_key, 6)
    for position, shards_of in cuts:
        steps = jnp.exp(jax.random.uniform(jax.random.fold_in(own, position), (shards_of,), jnp.float32, smallest / len(cuts), largest / len(cuts)))
        level = level * jnp.repeat(steps, dims[position] // shards_of).reshape([-1 if axis == position else 1 for axis in range(len(dims))])
    return level


def gaussian(stream_key, shape, deviation, bound, cuts=(), kind=jnp.bfloat16):
    values = deviation * jax.random.normal(stream_key, shape, jnp.float32)
    if cuts:
        values = values * shard_levels(stream_key, shape, cuts, -0.22, 0.18)
    return jnp.clip(values, -bound, bound).astype(kind)


def setup_inputs(seed: int = 0, part: int = 0) -> dict:
    key_list = jax.random.split(jax.random.key(seed), 8)
    own_keys = jax.random.split(jax.random.fold_in(key_list[7], part), 8)
    return {
        "tokens": gaussian(own_keys[0], (TOKENS, D), 1.0, 6.0, ((0, 4), (1, 4))),
        "proj_in": gaussian(key_list[1], (L, D), D ** -0.5, 0.09375, ((0, 4), (1, 4))),
        "proj_out": gaussian(key_list[2], (L, D), L ** -0.5, 0.1875, ((0, 4), (1, 4))),
        "expert_up": gaussian(key_list[3], (EXPERTS, L, FF), L ** -0.5, 0.1875, ((0, 16),)),
        "expert_down": gaussian(key_list[4], (EXPERTS, FF, L), FF ** -0.5, 0.125, ((0, 16),)),
        "expert_ids": draw_expert_ids(jax.random.fold_in(jax.random.fold_in(key_list[7], part), 71), part),
        "weight_codes": plant(jax.random.randint(own_keys[6], (TOKENS, PICKS), 1, 65), jax.random.fold_in(own_keys[6], 1), 1, 64).astype(jnp.int32),
    }


def reference(tokens, proj_in, proj_out, expert_up, expert_down, expert_ids, weight_codes):
    codes = weight_codes.astype(jnp.float32)
    route_weights = codes / jnp.sum(codes, axis=1, keepdims=True)
    latent = lax.dot_general(tokens, proj_in, (((1,), (1,)), ((), ())), preferred_element_type=jnp.float32).astype(jnp.bfloat16)
    flat_ids = expert_ids.reshape(-1).astype(jnp.int32)
    order = jnp.argsort(flat_ids, stable=True).astype(jnp.int32)
    sorted_ids = flat_ids[order]
    source_rows = (order // PICKS).astype(jnp.int32)
    block_rows = 128
    block_count = (TOKENS * PICKS) // block_rows

    def one_block(block):
        start = (block * block_rows).astype(jnp.int32)
        ids_here = lax.dynamic_slice_in_dim(sorted_ids, start, block_rows, 0)
        rows_here = lax.dynamic_slice_in_dim(source_rows, start, block_rows, 0)
        inputs = latent[rows_here]

        def apply_one(expert, accum):
            up_here = lax.dynamic_index_in_dim(expert_up, expert, 0, keepdims=False)
            down_here = lax.dynamic_index_in_dim(expert_down, expert, 0, keepdims=False)
            hidden = jnp.dot(inputs, up_here, preferred_element_type=jnp.float32)
            hidden = jnp.square(jnp.maximum(hidden, 0.0)).astype(jnp.bfloat16)
            result = jnp.dot(hidden, down_here, preferred_element_type=jnp.float32).astype(jnp.bfloat16)
            return jnp.where((ids_here == expert)[:, None], result, accum)

        empty = jnp.zeros((block_rows, L), jnp.bfloat16)
        return lax.fori_loop(ids_here[0], ids_here[block_rows - 1] + 1, apply_one, empty)

    outputs = lax.map(one_block, jnp.arange(block_count, dtype=jnp.int32)).reshape(TOKENS * PICKS, L)
    placed = jnp.zeros((TOKENS * PICKS, L), jnp.bfloat16).at[order].set(outputs).reshape(TOKENS, PICKS, L)
    combined = jnp.sum(route_weights[:, :, None] * placed.astype(jnp.float32), axis=1).astype(jnp.bfloat16)
    return jnp.dot(combined, proj_out, preferred_element_type=jnp.float32).astype(jnp.bfloat16)
```

```python
import functools

import jax
import jax.numpy as jnp
from jax import lax
from jax.experimental import pallas as pl
from jax.experimental.pallas import tpu as pltpu
from jax.sharding import PartitionSpec as P


def expert_block(arrived, expert_up, expert_down):
    width = arrived.shape[-1]
    flat_rows = arrived.reshape(-1, width)
    hidden = jnp.dot(flat_rows, expert_up[0], preferred_element_type=jnp.float32)
    hidden = jnp.square(jnp.maximum(hidden, 0.0)).astype(jnp.bfloat16)
    result = jnp.dot(hidden, expert_down[0], preferred_element_type=jnp.float32)
    return result.astype(jnp.bfloat16).reshape(arrived.shape)


def slot_positions(bucket, live, buckets):
    labels = jnp.arange(buckets, dtype=jnp.int32)
    onehot = jnp.logical_and(bucket[:, :, None] == labels, live[:, :, None]).astype(jnp.int32)
    per_row = jnp.sum(onehot, axis=1)
    before = jnp.cumsum(per_row, axis=0) - per_row
    return jnp.take_along_axis(before, bucket, axis=1)


def per_device(tokens, proj_in, proj_out, expert_up, expert_down, expert_ids, weight_codes):
    ep_count = lax.axis_size("ep")
    group_count = lax.axis_size("grp")
    experts = ep_count * group_count
    tok_block = tokens.shape[0]
    tok_dev = tok_block // group_count
    picks = expert_ids.shape[1]
    width = expert_up.shape[1]
    capacity = max(2, (4 * tok_dev * picks + 3 * experts - 1) // (3 * experts))
    in_rows, out_rows = (
        lax.all_gather(proj_in, "ep", axis=0, tiled=True),
        lax.all_gather(proj_out, "ep", axis=0, tiled=True),
    )
    latent = lax.psum_scatter(
        lax.dot_general(
            tokens, in_rows, (((1,), (1,)), ((), ())), preferred_element_type=jnp.float32
        ),
        "grp",
        scatter_dimension=0,
        tiled=True,
    ).astype(jnp.bfloat16)
    codes = weight_codes.astype(jnp.float32)
    route_weights = codes / jnp.sum(codes, axis=1, keepdims=True)
    group_index = lax.axis_index("grp")
    my_ids = lax.dynamic_slice_in_dim(expert_ids, group_index * tok_dev, tok_dev, 0)
    my_weights = lax.dynamic_slice_in_dim(route_weights, group_index * tok_dev, tok_dev, 0)
    position = slot_positions(my_ids, jnp.ones(my_ids.shape, jnp.bool_), experts)
    spread = jnp.broadcast_to(latent[:, None, :], (tok_dev, picks, width))
    outgoing = jnp.zeros((experts, capacity, width), jnp.bfloat16).at[my_ids, position].set(spread)
    computed = expert_block(
        lax.all_to_all(outgoing, ("ep", "grp"), split_axis=0, concat_axis=0, tiled=True),
        expert_up,
        expert_down,
    )
    returned = lax.all_to_all(computed, ("ep", "grp"), split_axis=0, concat_axis=0, tiled=True)
    picked = returned[my_ids, position]
    combined = jnp.sum(my_weights[:, :, None] * picked.astype(jnp.float32), axis=1)
    latent_out = combined.astype(jnp.bfloat16)
    mixed = jnp.dot(
        lax.all_gather(latent_out, "grp", axis=0, tiled=True),
        out_rows,
        preferred_element_type=jnp.float32,
    )
    return mixed.astype(jnp.bfloat16)


MESH = pl.DeviceIdType.MESH
BF = jnp.bfloat16
F32 = jnp.float32


def nt(a, b):
    return lax.dot_general(a, b, (((1,), (1,)), ((), ())), preferred_element_type=F32)


def nn(a, b):
    return jnp.dot(a, b, preferred_element_type=F32)


def fused_kernel(
    groups, blocks, hits, cap,
    tok, pin, pout, routing, up_hbm, down_hbm, out,
    up, down, win, wout, meta, onehot_t, onehot, inv,
    own, r1, l1, sr1, sl1, lat, xs, xin, hid, ys, mates, zsum, yret, sown, r2, l2, sr2, sl2,
    hbm_sem, ag_s, ag_r, r1s, r1r, l1s, l1r, xss, xsr, ms, mr, yss, ysr, r2s, r2r, l2s, l2r,
):
    ep, z = lax.axis_index("ep"), lax.axis_index("grp")
    chip = ep // 2
    mate = chip * 2 + (1 - ep % 2)
    ypart = (ep + 2) % 4
    rows = tok.shape[0] // blocks
    half = own.shape[2]
    picks = routing.shape[0] // 2
    far = jnp.maximum(z, groups - 1 - z)

    def rcopy(src, dst, s, r, **dev):
        return pltpu.make_async_remote_copy(
            src_ref=src, dst_ref=dst, send_sem=s, recv_sem=r, device_id=dev, device_id_type=MESH
        )

    loads = [
        pltpu.make_async_copy(up_hbm.at[0], up, hbm_sem.at[0]),
        pltpu.make_async_copy(down_hbm.at[0], down, hbm_sem.at[1]),
    ]

    barrier = pltpu.get_barrier_semaphore()
    for peer in (mate, ypart):
        pl.semaphore_signal(barrier, inc=1, device_id={"ep": peer}, device_id_type=MESH)

    @pl.when(z > 0)
    def _():
        pl.semaphore_signal(barrier, inc=1, device_id={"grp": z - 1}, device_id_type=MESH)

    @pl.when(z < groups - 1)
    def _():
        pl.semaphore_signal(barrier, inc=1, device_id={"grp": z + 1}, device_id_type=MESH)

    inner = jnp.logical_and(z > 0, z < groups - 1)
    pl.semaphore_wait(barrier, jnp.where(inner, 4, 3))

    def ag(kind, src, buf, at_own, at_y, mine_y, mine_mate, relay_to):
        to_y = rcopy(src, buf.at[mine_y], ag_s.at[kind, 0], ag_r.at[kind, 0], ep=ypart)
        to_mate = rcopy(src, buf.at[mine_mate], ag_s.at[kind, 1], ag_r.at[kind, 1], ep=mate)
        relay = rcopy(buf.at[at_y], buf.at[relay_to], ag_s.at[kind, 2], ag_r.at[kind, 2], ep=mate)
        return to_y, to_mate, relay

    win_y, win_m, win_relay = ag(0, pin, win, ep, ypart, ep, ep, ypart)
    wout_y, wout_m, wout_relay = ag(1, pout, wout, ep, ypart, ep, ep, ypart)
    meta_y, meta_m, meta_relay = ag(2, meta.at[0], meta, 0, 1, 1, 2, 3)
    win_y.start()
    win_m.start()
    for load in loads:
        load.start()

    ids = routing[0:picks, :]
    codes = routing[picks : 2 * picks, :].astype(F32)
    experts_here = lax.broadcasted_iota(jnp.int32, (8, ids.shape[1]), 0) * groups + z
    table = jnp.zeros((8, ids.shape[1]), F32)
    for p in range(picks):
        table = table + jnp.where(ids[p : p + 1, :] == experts_here, codes[p : p + 1, :], 0.0)
    inverse = 1.0 / jnp.sum(codes, axis=0, keepdims=True)
    hit = jnp.where(jnp.sum(table, axis=0, keepdims=True) > 0.0, 1.0, 0.0)

    def before(n):
        i = lax.broadcasted_iota(jnp.int32, (n, n), 0)
        j = lax.broadcasted_iota(jnp.int32, (n, n), 1)
        return jnp.where(i < j, 1.0, 0.0).astype(BF)

    def ranked(sel, count):
        n = sel.shape[1]
        rank = nn(jnp.broadcast_to(sel, (8, n)).astype(BF), before(n))[0:1, :]
        slot = lax.broadcasted_iota(jnp.int32, (count, n), 0).astype(F32)
        return jnp.where(jnp.logical_and(slot == rank, sel > 0.0), 1.0, 0.0)

    for b in range(blocks):
        at = slice(b * rows, (b + 1) * rows)
        chosen = ranked(hit[:, at], hits)
        onehot[b] = chosen.astype(BF)
        onehot_t[b] = jnp.transpose(chosen).astype(BF)
        meta[0, b] = nt(table[:, at].astype(BF), chosen.astype(BF))
        inv[b] = jnp.transpose(jnp.broadcast_to(inverse[:, at], (rows, rows)))
    meta_y.start()
    meta_m.start()

    win[ep] = pin[...]
    wout[ep] = pout[...]
    win_m.wait_recv()

    def partial(h):
        w = win[pl.ds(2 * jnp.where(h == 0, chip, 1 - chip), 2)].reshape(half, win.shape[2])
        for b in range(blocks):
            own[h * blocks + b] = nt(tok[b * rows : (b + 1) * rows, :], w)

    def hop(k, recv, send, s, r, first, last, dest, mine):
        @pl.when(jnp.logical_not(first))
        def _():
            rcopy(send.at[k], recv.at[k], s.at[k], r.at[k], grp=dest).wait_recv()

        @pl.when(jnp.logical_not(last))
        def _():
            @pl.when(first)
            def _():
                send[k] = mine[k].astype(BF)

            @pl.when(jnp.logical_not(first))
            def _():
                send[k] = (mine[k].astype(F32) + recv[k].astype(F32)).astype(BF)

            rcopy(send.at[k], recv.at[k], s.at[k], r.at[k], grp=dest).start()

    right = jnp.minimum(z + 1, groups - 1)
    left = jnp.maximum(z - 1, 0)

    def hops(t, n, bufs, mine):
        rr, ll, ss, sl, rs_, rr_, ls_, lr_ = bufs
        kr, kl = t - z, t - (groups - 1 - z)

        @pl.when(jnp.logical_and(kr >= 0, kr < n))
        def _():
            hop(kr, rr, ss, rs_, rr_, z == 0, z == groups - 1, right, mine)

        @pl.when(jnp.logical_and(kl >= 0, kl < n))
        def _():
            hop(kl, ll, sl, ls_, lr_, z == groups - 1, z == 0, left, mine)

    def total(k, rr, ll, mine, finish):
        @pl.when(z == 0)
        def _():
            finish(mine[k].astype(F32) + ll[k].astype(F32))

        @pl.when(z == groups - 1)
        def _():
            finish(mine[k].astype(F32) + rr[k].astype(F32))

        @pl.when(jnp.logical_and(z > 0, z < groups - 1))
        def _():
            finish(mine[k].astype(F32) + rr[k].astype(F32) + ll[k].astype(F32))

    def x_copies(b):
        return (
            rcopy(xs.at[b, 0], xs.at[b, 1], xss.at[b, 0], xsr.at[b, 0], ep=ypart),
            rcopy(xs.at[b, 0], xs.at[b, 2], xss.at[b, 1], xsr.at[b, 1], ep=mate),
            rcopy(xs.at[b, 1], xs.at[b, 3], xss.at[b, 2], xsr.at[b, 2], ep=mate),
        )

    bufs1 = (r1, l1, sr1, sl1, r1s, r1r, l1s, l1r)
    chunks = 2 * blocks

    def step1(t, _):
        hops(t, chunks, bufs1, own)
        k = t - far

        @pl.when(jnp.logical_and(k >= 0, k < chunks))
        def _():
            h = k // blocks
            b = k % blocks
            column = pl.multiple_of(jnp.where(h == 0, chip, 1 - chip) * half, half)

            def finish(v):
                lat[b, :, pl.ds(column, half)] = v.astype(BF)

            total(k, r1, l1, own, finish)

            @pl.when(h == 1)
            def _():
                xs[b, 0] = nn(onehot[b], lat[b]).astype(BF)
                a, c, _ = x_copies(b)
                a.start()
                c.start()

        return 0

    partial(0)
    lax.fori_loop(0, blocks, step1, 0)
    win_y.wait_recv()
    win_relay.start()
    meta_y.wait_recv()
    meta_relay.start()
    wout_m.start()
    wout_y.start()
    win_relay.wait_recv()
    partial(1)
    lax.fori_loop(blocks, chunks + groups - 1, step1, 0)
    for load in loads:
        load.wait()
    meta_m.wait_recv()
    meta_relay.wait_recv()

    def m_copy(b):
        return rcopy(ys.at[b, pl.ds(2, 2)], mates.at[b], ms.at[b], mr.at[b], ep=mate)

    def y_copy(b):
        return rcopy(zsum.at[b, 1], yret.at[b], yss.at[b], ysr.at[b], ep=ypart)

    bufs2 = (r2, l2, sr2, sl2, r2s, r2r, l2s, l2r)

    def step2(u, _):
        @pl.when(u < blocks)
        def _():
            b = u
            a, c, relay = x_copies(b)
            a.wait_recv()
            relay.start()
            c.wait_recv()
            relay.wait_recv()
            scaled = []
            for s in range(4):
                m = meta[s, b, pl.ds(ep, 1), :]
                q = ranked(jnp.where(m > 0.0, 1.0, 0.0), cap)
                xin[s * cap : (s + 1) * cap, :] = nn(q.astype(BF), xs[b, s]).astype(BF)
                scaled.append(jnp.transpose(q * m).astype(BF))
            h = jnp.maximum(nn(xin[...], up[...]), 0.0)
            hid[...] = (h * h).astype(BF)
            o = nn(hid[...], down[...]).astype(BF)
            for s in range(4):
                ys[b, s] = nn(scaled[s], o[s * cap : (s + 1) * cap, :]).astype(BF)
            m_copy(b).start()

        @pl.when(jnp.logical_and(u >= 1, u < blocks + 1))
        def _():
            b = u - 1
            m_copy(b).wait_recv()
            zsum[b] = (ys[b, 0:2].astype(F32) + mates[b].astype(F32)).astype(BF)
            y_copy(b).start()

        @pl.when(u == 1)
        def _():
            wout_y.wait_recv()
            wout_relay.start()

        @pl.when(jnp.logical_and(u >= 2, u < blocks + 2))
        def _():
            b = u - 2
            y_copy(b).wait_recv()
            v = (zsum[b, 0].astype(F32) + yret[b].astype(F32)).astype(BF)
            sown[b] = nn(onehot_t[b], v).astype(BF)

        @pl.when(u == 3)
        def _():
            wout_m.wait_recv()
            wout_relay.wait_recv()

        t = u - 2
        hops(t, blocks, bufs2, sown)
        k = t - far

        @pl.when(jnp.logical_and(k >= 0, k < blocks))
        def _():
            def finish(v):
                w = jnp.concatenate([inv[k]] * (v.shape[1] // rows), axis=1)
                y = (v * w).astype(BF)
                full = wout[...].reshape(v.shape[1], wout.shape[2])
                out[pl.ds(pl.multiple_of(k * rows, rows), rows), :] = nn(y, full).astype(BF)

            total(k, r2, l2, sown, finish)

        return 0

    lax.fori_loop(0, blocks + 2 + groups - 1, step2, 0)

    for copy in (win_y, win_m, win_relay, wout_y, wout_m, wout_relay, meta_y, meta_m, meta_relay):
        copy.wait_send()

    def drain(n, bufs):
        rr, ll, ss, sl, rs_, rr_, ls_, lr_ = bufs

        @pl.when(z < groups - 1)
        def _():
            for k in range(n):
                rcopy(ss.at[k], rr.at[k], rs_.at[k], rr_.at[k], grp=right).wait_send()

        @pl.when(z > 0)
        def _():
            for k in range(n):
                rcopy(sl.at[k], ll.at[k], ls_.at[k], lr_.at[k], grp=left).wait_send()

    drain(chunks, bufs1)
    drain(blocks, bufs2)
    for b in range(blocks):
        for copy in x_copies(b):
            copy.wait_send()
        m_copy(b).wait_send()
        y_copy(b).wait_send()


def fused_device(sizes, tokens, proj_in, proj_out, expert_up, expert_down, expert_ids, weight_codes):
    groups = sizes["grp"]
    blocks = groups
    rows = tokens.shape[0] // blocks
    picks = expert_ids.shape[1]
    experts = sizes["ep"] * groups
    hits = rows * (picks // 2) // groups
    cap = max(2, (4 * rows * picks + 3 * experts - 1) // (3 * experts))
    latent, features = proj_in.shape[0] * sizes["ep"], proj_in.shape[1]
    hidden = expert_up.shape[2]
    half = latent // 2
    routing = jnp.concatenate([expert_ids.T, weight_codes.T], axis=0)
    chunks = 2 * blocks
    vm = pltpu.VMEM
    dma = pltpu.SemaphoreType.DMA
    scratch = [
        vm((latent, hidden), BF), vm((hidden, latent), BF),
        vm((4, *proj_in.shape), BF), vm((4, *proj_out.shape), BF),
        vm((4, blocks, 8, hits), F32), vm((blocks, rows, hits), BF), vm((blocks, hits, rows), BF),
        vm((blocks, rows, rows), F32),
        vm((chunks, rows, half), F32),
        *[vm((chunks, rows, half), BF)] * 4,
        vm((blocks, rows, latent), BF),
        vm((blocks, 4, hits, latent), BF),
        vm((4 * cap, latent), BF), vm((4 * cap, hidden), BF),
        vm((blocks, 4, hits, latent), BF),
        vm((blocks, 2, hits, latent), BF), vm((blocks, 2, hits, latent), BF),
        vm((blocks, hits, latent), BF),
        vm((blocks, rows, latent), BF),
        *[vm((blocks, rows, latent), BF)] * 4,
        dma((2,)), dma((3, 3)), dma((3, 3)),
        *[dma((chunks,))] * 4,
        dma((blocks, 3)), dma((blocks, 3)),
        *[dma((blocks,))] * 8,
    ]
    vmem = pl.BlockSpec(memory_space=pltpu.VMEM)
    hbm = pl.BlockSpec(memory_space=pl.ANY)
    return pl.pallas_call(
        functools.partial(fused_kernel, groups, blocks, hits, cap),
        out_shape=jax.ShapeDtypeStruct((tokens.shape[0], features), BF),
        in_specs=[vmem, vmem, vmem, vmem, hbm, hbm],
        out_specs=vmem,
        scratch_shapes=scratch,
        compiler_params=pltpu.CompilerParams(
            collective_id=0, has_side_effects=True, vmem_limit_bytes=60 << 20
        ),
    )(tokens, proj_in, proj_out, routing, expert_up, expert_down)


def solution(mesh):
    sizes = dict(mesh.shape)
    body = per_device
    if sizes["ep"] == 4 and sizes["grp"] <= 4:
        body = functools.partial(fused_device, sizes)
    in_specs = (
        P(("rep", "ep"), "grp"),
        P("ep", "grp"),
        P("ep", "grp"),
        P(("ep", "grp"), None, None),
        P(("ep", "grp"), None, None),
        P(("rep", "ep"), None),
        P(("rep", "ep"), None),
    )
    out_specs = P(("rep", "ep"), "grp")
    return jax.shard_map(
        body, mesh=mesh, in_specs=in_specs, out_specs=out_specs, check_vma=False
    )
```

```python
import functools

import jax
import jax.numpy as jnp
from jax import lax
from jax.experimental import pallas as pl
from jax.experimental.pallas import tpu as pltpu
from jax.sharding import PartitionSpec as P


def expert_block(arrived, expert_up, expert_down):
    width = arrived.shape[-1]
    flat_rows = arrived.reshape(-1, width)
    hidden = jnp.dot(flat_rows, expert_up[0], preferred_element_type=jnp.float32)
    hidden = jnp.square(jnp.maximum(hidden, 0.0)).astype(jnp.bfloat16)
    result = jnp.dot(hidden, expert_down[0], preferred_element_type=jnp.float32)
    return result.astype(jnp.bfloat16).reshape(arrived.shape)


def slot_positions(bucket, live, buckets):
    labels = jnp.arange(buckets, dtype=jnp.int32)
    onehot = jnp.logical_and(bucket[:, :, None] == labels, live[:, :, None]).astype(jnp.int32)
    per_row = jnp.sum(onehot, axis=1)
    before = jnp.cumsum(per_row, axis=0) - per_row
    return jnp.take_along_axis(before, bucket, axis=1)


def per_device(tokens, proj_in, proj_out, expert_up, expert_down, expert_ids, weight_codes):
    ep_count = lax.axis_size("ep")
    group_count = lax.axis_size("grp")
    experts = ep_count * group_count
    tok_block = tokens.shape[0]
    tok_dev = tok_block // group_count
    picks = expert_ids.shape[1]
    width = expert_up.shape[1]
    capacity = max(2, (4 * tok_dev * picks + 3 * experts - 1) // (3 * experts))
    in_rows, out_rows = (
        lax.all_gather(proj_in, "ep", axis=0, tiled=True),
        lax.all_gather(proj_out, "ep", axis=0, tiled=True),
    )
    latent = lax.psum_scatter(
        lax.dot_general(
            tokens, in_rows, (((1,), (1,)), ((), ())), preferred_element_type=jnp.float32
        ),
        "grp",
        scatter_dimension=0,
        tiled=True,
    ).astype(jnp.bfloat16)
    codes = weight_codes.astype(jnp.float32)
    route_weights = codes / jnp.sum(codes, axis=1, keepdims=True)
    group_index = lax.axis_index("grp")
    my_ids = lax.dynamic_slice_in_dim(expert_ids, group_index * tok_dev, tok_dev, 0)
    my_weights = lax.dynamic_slice_in_dim(route_weights, group_index * tok_dev, tok_dev, 0)
    position = slot_positions(my_ids, jnp.ones(my_ids.shape, jnp.bool_), experts)
    spread = jnp.broadcast_to(latent[:, None, :], (tok_dev, picks, width))
    outgoing = jnp.zeros((experts, capacity, width), jnp.bfloat16).at[my_ids, position].set(spread)
    computed = expert_block(
        lax.all_to_all(outgoing, ("ep", "grp"), split_axis=0, concat_axis=0, tiled=True),
        expert_up,
        expert_down,
    )
    returned = lax.all_to_all(computed, ("ep", "grp"), split_axis=0, concat_axis=0, tiled=True)
    picked = returned[my_ids, position]
    combined = jnp.sum(my_weights[:, :, None] * picked.astype(jnp.float32), axis=1)
    latent_out = combined.astype(jnp.bfloat16)
    mixed = jnp.dot(
        lax.all_gather(latent_out, "grp", axis=0, tiled=True),
        out_rows,
        preferred_element_type=jnp.float32,
    )
    return mixed.astype(jnp.bfloat16)


MESH = pl.DeviceIdType.MESH
BF = jnp.bfloat16
F32 = jnp.float32


def nt(a, b):
    return lax.dot_general(a, b, (((1,), (1,)), ((), ())), preferred_element_type=F32)


def nn(a, b):
    return jnp.dot(a, b, preferred_element_type=F32)


def fused_kernel(
    groups, blocks, hits, cap,
    tok, pin, pout, routing, up_hbm, down_hbm, out,
    up, down, win, wout, meta, onehot_t, onehot, inv,
    own, r1, l1, sr1, sl1, lat, xs, xin, hid, ys, mates, zsum, yret, sown, r2, l2, sr2, sl2,
    hbm_sem, ag_s, ag_r, r1s, r1r, l1s, l1r, xss, xsr, ms, mr, yss, ysr, r2s, r2r, l2s, l2r,
):
    ep, z, part = lax.axis_index("ep"), lax.axis_index("grp"), lax.axis_index("rep")
    chip = ep // 2
    mate = chip * 2 + (1 - ep % 2)
    ypart = (ep + 2) % 4
    rows = tok.shape[0] // blocks
    half = own.shape[2]
    picks = routing.shape[0] // 2
    far = jnp.maximum(z, groups - 1 - z)

    def rcopy(src, dst, s, r, **dev):
        return pltpu.make_async_remote_copy(
            src_ref=src, dst_ref=dst, send_sem=s, recv_sem=r, device_id=dev, device_id_type=MESH
        )

    loads = [
        pltpu.make_async_copy(up_hbm.at[0], up, hbm_sem.at[0]),
        pltpu.make_async_copy(down_hbm.at[0], down, hbm_sem.at[1]),
    ]

    barrier = pltpu.get_barrier_semaphore()
    for peer in (mate, ypart):
        pl.semaphore_signal(barrier, inc=1, device_id={"ep": peer}, device_id_type=MESH)
    pl.semaphore_signal(barrier, inc=1, device_id={"rep": 1 - part}, device_id_type=MESH)

    @pl.when(z > 0)
    def _():
        pl.semaphore_signal(barrier, inc=1, device_id={"grp": z - 1}, device_id_type=MESH)

    @pl.when(z < groups - 1)
    def _():
        pl.semaphore_signal(barrier, inc=1, device_id={"grp": z + 1}, device_id_type=MESH)

    inner = jnp.logical_and(z > 0, z < groups - 1)
    pl.semaphore_wait(barrier, jnp.where(inner, 5, 4))

    share = pin.shape[0] // 2
    my_share = pl.ds(pl.multiple_of(part * share, share), share)
    peer_share = pl.ds(pl.multiple_of((1 - part) * share, share), share)

    def ag(kind, src, buf):
        def one(i, a, b, **dev):
            return rcopy(a, b, ag_s.at[kind, i], ag_r.at[kind, i], **dev)

        first, second = buf.at[ypart, my_share], buf.at[ypart, peer_share]
        return (
            one(0, src.at[my_share], buf.at[ep, my_share], ep=ypart),
            one(1, src, buf.at[ep], ep=mate),
            one(2, first, first, ep=mate),
            one(3, first, first, rep=1 - part),
            one(4, second, second, ep=mate),
        )

    win_y, win_m, win_relay, win_x, win_relay2 = ag(0, pin, win)
    wout_y, wout_m, wout_relay, wout_x, wout_relay2 = ag(1, pout, wout)
    meta_y = rcopy(meta.at[0], meta.at[1], ag_s.at[2, 0], ag_r.at[2, 0], ep=ypart)
    meta_m = rcopy(meta.at[0], meta.at[2], ag_s.at[2, 1], ag_r.at[2, 1], ep=mate)
    meta_relay = rcopy(meta.at[1], meta.at[3], ag_s.at[2, 2], ag_r.at[2, 2], ep=mate)
    win_y.start()
    win_m.start()
    for load in loads:
        load.start()

    ids = routing[0:picks, :]
    codes = routing[picks : 2 * picks, :].astype(F32)
    experts_here = lax.broadcasted_iota(jnp.int32, (8, ids.shape[1]), 0) * groups + z
    table = jnp.zeros((8, ids.shape[1]), F32)
    for p in range(picks):
        table = table + jnp.where(ids[p : p + 1, :] == experts_here, codes[p : p + 1, :], 0.0)
    inverse = 1.0 / jnp.sum(codes, axis=0, keepdims=True)
    hit = jnp.where(jnp.sum(table, axis=0, keepdims=True) > 0.0, 1.0, 0.0)

    def before(n):
        i = lax.broadcasted_iota(jnp.int32, (n, n), 0)
        j = lax.broadcasted_iota(jnp.int32, (n, n), 1)
        return jnp.where(i < j, 1.0, 0.0).astype(BF)

    def ranked(sel, count):
        n = sel.shape[1]
        rank = nn(jnp.broadcast_to(sel, (8, n)).astype(BF), before(n))[0:1, :]
        slot = lax.broadcasted_iota(jnp.int32, (count, n), 0).astype(F32)
        return jnp.where(jnp.logical_and(slot == rank, sel > 0.0), 1.0, 0.0)

    for b in range(blocks):
        at = slice(b * rows, (b + 1) * rows)
        chosen = ranked(hit[:, at], hits)
        onehot[b] = chosen.astype(BF)
        onehot_t[b] = jnp.transpose(chosen).astype(BF)
        meta[0, b] = nt(table[:, at].astype(BF), chosen.astype(BF))
        inv[b] = jnp.transpose(jnp.broadcast_to(inverse[:, at], (rows, rows)))
    meta_y.start()
    meta_m.start()

    win[ep] = pin[...]
    wout[ep] = pout[...]
    win_m.wait_recv()

    def partial(h):
        w = win[pl.ds(2 * jnp.where(h == 0, chip, 1 - chip), 2)].reshape(half, win.shape[2])
        for b in range(blocks):
            own[2 * (b // 2) * 2 + 2 * h + b % 2] = nt(tok[b * rows : (b + 1) * rows, :], w)

    def hop(k, recv, send, s, r, first, last, dest, mine):
        @pl.when(jnp.logical_not(first))
        def _():
            rcopy(send.at[k], recv.at[k], s.at[k], r.at[k], grp=dest).wait_recv()

        @pl.when(jnp.logical_not(last))
        def _():
            @pl.when(first)
            def _():
                send[k] = mine[k].astype(BF)

            @pl.when(jnp.logical_not(first))
            def _():
                send[k] = (mine[k].astype(F32) + recv[k].astype(F32)).astype(BF)

            rcopy(send.at[k], recv.at[k], s.at[k], r.at[k], grp=dest).start()

    right = jnp.minimum(z + 1, groups - 1)
    left = jnp.maximum(z - 1, 0)

    def hops(t, n, bufs, mine):
        rr, ll, ss, sl, rs_, rr_, ls_, lr_ = bufs
        kr, kl = t - z, t - (groups - 1 - z)

        @pl.when(jnp.logical_and(kr >= 0, kr < n))
        def _():
            hop(kr, rr, ss, rs_, rr_, z == 0, z == groups - 1, right, mine)

        @pl.when(jnp.logical_and(kl >= 0, kl < n))
        def _():
            hop(kl, ll, sl, ls_, lr_, z == groups - 1, z == 0, left, mine)

    def total(k, rr, ll, mine, finish):
        @pl.when(z == 0)
        def _():
            finish(mine[k].astype(F32) + ll[k].astype(F32))

        @pl.when(z == groups - 1)
        def _():
            finish(mine[k].astype(F32) + rr[k].astype(F32))

        @pl.when(jnp.logical_and(z > 0, z < groups - 1))
        def _():
            finish(mine[k].astype(F32) + rr[k].astype(F32) + ll[k].astype(F32))

    def x_copies(b):
        return (
            rcopy(xs.at[b, 0], xs.at[b, 1], xss.at[b, 0], xsr.at[b, 0], ep=ypart),
            rcopy(xs.at[b, 0], xs.at[b, 2], xss.at[b, 1], xsr.at[b, 1], ep=mate),
            rcopy(xs.at[b, 1], xs.at[b, 3], xss.at[b, 2], xsr.at[b, 2], ep=mate),
        )

    bufs1 = (r1, l1, sr1, sl1, r1s, r1r, l1s, l1r)
    chunks = 2 * blocks

    def step1(t, _):
        hops(t, chunks, bufs1, own)
        k = t - far

        @pl.when(jnp.logical_and(k >= 0, k < chunks))
        def _():
            h = k % 4 // 2
            b = k // 4 * 2 + k % 2
            column = pl.multiple_of(jnp.where(h == 0, chip, 1 - chip) * half, half)

            def finish(v):
                lat[b, :, pl.ds(column, half)] = v.astype(BF)

            total(k, r1, l1, own, finish)

            @pl.when(h == 1)
            def _():
                xs[b, 0] = nn(onehot[b], lat[b]).astype(BF)
                a, c, _ = x_copies(b)
                a.start()
                c.start()

        return 0

    def m_copy(b):
        return rcopy(ys.at[b, pl.ds(2, 2)], mates.at[b], ms.at[b], mr.at[b], ep=mate)

    def y_copy(b):
        return rcopy(zsum.at[b, 1], yret.at[b], yss.at[b], ysr.at[b], ep=ypart)

    bufs2 = (r2, l2, sr2, sl2, r2s, r2r, l2s, l2r)

    def relay_x(b):
        a, _, relay = x_copies(b)
        a.wait_recv()
        relay.start()

    def expert(b):
        _, c, relay = x_copies(b)
        c.wait_recv()
        relay.wait_recv()
        scaled = []
        for s in range(4):
            m = meta[s, b, pl.ds(ep, 1), :]
            q = ranked(jnp.where(m > 0.0, 1.0, 0.0), cap)
            xin[s * cap : (s + 1) * cap, :] = nn(q.astype(BF), xs[b, s]).astype(BF)
            scaled.append(jnp.transpose(q * m).astype(BF))
        h = jnp.maximum(nn(xin[...], up[...]), 0.0)
        hid[...] = (h * h).astype(BF)
        o = nn(hid[...], down[...]).astype(BF)
        for s in (2, 3, 0, 1):
            ys[b, s] = nn(scaled[s], o[s * cap : (s + 1) * cap, :]).astype(BF)
            if s == 3:
                m_copy(b).start()

    def pair(b):
        m_copy(b).wait_recv()
        zsum[b, 1] = (ys[b, 1].astype(F32) + mates[b, 1].astype(F32)).astype(BF)
        y_copy(b).start()
        zsum[b, 0] = (ys[b, 0].astype(F32) + mates[b, 0].astype(F32)).astype(BF)

    def home(b):
        y_copy(b).wait_recv()
        v = (zsum[b, 0].astype(F32) + yret[b].astype(F32)).astype(BF)
        for c in range(2):
            sown[2 * b + c] = nn(onehot_t[b], v[:, c * half : (c + 1) * half]).astype(BF)

    def step2(t, _):
        hops(t, chunks, bufs2, sown)
        k = t - far

        @pl.when(jnp.logical_and(k >= 0, k < chunks))
        def _():
            b = k // 2
            column = pl.multiple_of(k % 2 * half, half)

            def finish(v):
                w = jnp.concatenate([inv[b]] * (half // rows), axis=1)
                lat[b, :, pl.ds(column, half)] = (v * w).astype(BF)

            total(k, r2, l2, sown, finish)

            @pl.when(k % 2 == 1)
            def _():
                full = wout[...].reshape(2 * half, wout.shape[2])
                out[pl.ds(pl.multiple_of(b * rows, rows), rows), :] = nn(lat[b], full).astype(BF)

        return 0

    partial(0)
    lax.fori_loop(0, 2, step1, 0)
    win_y.wait_recv()
    win_relay.start()
    win_x.start()
    meta_y.wait_recv()
    meta_relay.start()
    wout_m.start()
    wout_y.start()
    win_x.wait_recv()
    win_relay2.start()
    win_relay.wait_recv()
    win_relay2.wait_recv()
    partial(1)
    steps = chunks + groups - 1
    lax.fori_loop(2, 7, step1, 0)
    relay_x(0)
    lax.fori_loop(7, 8, step1, 0)
    for load in loads:
        load.wait()
    meta_m.wait_recv()
    meta_relay.wait_recv()
    expert(0)
    relay_x(1)
    pair(0)
    lax.fori_loop(8, steps, step1, 0)
    wout_y.wait_recv()
    wout_relay.start()
    wout_x.start()
    for b in range(1, blocks):
        expert(b)
        if b == 1:
            wout_x.wait_recv()
            wout_relay2.start()
        if b + 1 < blocks:
            relay_x(b + 1)
        home(b - 1)
        if b == 2:
            wout_m.wait_recv()
            wout_relay.wait_recv()
            wout_relay2.wait_recv()
        lax.fori_loop(2 * (b - 1), 2 * b, step2, 0)
        pair(b)
    home(blocks - 1)
    lax.fori_loop(2 * (blocks - 1), steps, step2, 0)

    for copy in (
        *(win_y, win_m, win_relay, win_x, win_relay2),
        *(wout_y, wout_m, wout_relay, wout_x, wout_relay2),
        *(meta_y, meta_m, meta_relay),
    ):
        copy.wait_send()

    def drain(n, bufs):
        rr, ll, ss, sl, rs_, rr_, ls_, lr_ = bufs

        @pl.when(z < groups - 1)
        def _():
            for k in range(n):
                rcopy(ss.at[k], rr.at[k], rs_.at[k], rr_.at[k], grp=right).wait_send()

        @pl.when(z > 0)
        def _():
            for k in range(n):
                rcopy(sl.at[k], ll.at[k], ls_.at[k], lr_.at[k], grp=left).wait_send()

    drain(chunks, bufs1)
    drain(chunks, bufs2)
    for b in range(blocks):
        for copy in x_copies(b):
            copy.wait_send()
        m_copy(b).wait_send()
        y_copy(b).wait_send()


def fused_device(sizes, tokens, proj_in, proj_out, expert_up, expert_down, expert_ids, weight_codes):
    groups = sizes["grp"]
    blocks = groups
    rows = tokens.shape[0] // blocks
    picks = expert_ids.shape[1]
    experts = sizes["ep"] * groups
    hits = rows * (picks // 2) // groups
    cap = max(2, (4 * rows * picks + 3 * experts - 1) // (3 * experts))
    latent, features = proj_in.shape[0] * sizes["ep"], proj_in.shape[1]
    hidden = expert_up.shape[2]
    half = latent // 2
    routing = jnp.concatenate([expert_ids.T, weight_codes.T], axis=0)
    chunks = 2 * blocks
    vm = pltpu.VMEM
    dma = pltpu.SemaphoreType.DMA
    scratch = [
        vm((latent, hidden), BF), vm((hidden, latent), BF),
        vm((4, *proj_in.shape), BF), vm((4, *proj_out.shape), BF),
        vm((4, blocks, 8, hits), F32), vm((blocks, rows, hits), BF), vm((blocks, hits, rows), BF),
        vm((blocks, rows, rows), F32),
        vm((chunks, rows, half), F32),
        *[vm((chunks, rows, half), BF)] * 4,
        vm((blocks, rows, latent), BF),
        vm((blocks, 4, hits, latent), BF),
        vm((4 * cap, latent), BF), vm((4 * cap, hidden), BF),
        vm((blocks, 4, hits, latent), BF),
        vm((blocks, 2, hits, latent), BF), vm((blocks, 2, hits, latent), BF),
        vm((blocks, hits, latent), BF),
        *[vm((chunks, rows, half), BF)] * 5,
        dma((2,)), dma((3, 5)), dma((3, 5)),
        *[dma((chunks,))] * 4,
        dma((blocks, 3)), dma((blocks, 3)),
        *[dma((blocks,))] * 4,
        *[dma((chunks,))] * 4,
    ]
    vmem = pl.BlockSpec(memory_space=pltpu.VMEM)
    hbm = pl.BlockSpec(memory_space=pl.ANY)
    return pl.pallas_call(
        functools.partial(fused_kernel, groups, blocks, hits, cap),
        out_shape=jax.ShapeDtypeStruct((tokens.shape[0], features), BF),
        in_specs=[vmem, vmem, vmem, vmem, hbm, hbm],
        out_specs=vmem,
        scratch_shapes=scratch,
        compiler_params=pltpu.CompilerParams(
            collective_id=0, has_side_effects=True, vmem_limit_bytes=60 << 20
        ),
    )(tokens, proj_in, proj_out, routing, expert_up, expert_down)


def solution(mesh):
    sizes = dict(mesh.shape)
    body = per_device
    if sizes["rep"] == 2 and sizes["ep"] == 4 and sizes["grp"] == 4:
        body = functools.partial(fused_device, sizes)
    in_specs = (
        P(("rep", "ep"), "grp"),
        P("ep", "grp"),
        P("ep", "grp"),
        P(("ep", "grp"), None, None),
        P(("ep", "grp"), None, None),
        P(("rep", "ep"), None),
        P(("rep", "ep"), None),
    )
    out_specs = P(("rep", "ep"), "grp")
    return jax.shard_map(
        body, mesh=mesh, in_specs=in_specs, out_specs=out_specs, check_vma=False
    )
```
